32 devices in a mesh: lon: 8 (over y, x, core), lat: 4 (over z).
Axes of the slice: x: 2, y: 2, z: 4, core: 2. Of those that a mesh axis runs over, the one named last changes fastest.
Arguments:
- initial_kelvin_map: float32 [512, 256, 128], P('lon', 'lat'), may hold values from -6 to 6
- thermal_diffusivity_map: float32 [512, 256, 128], P('lon', 'lat'), may hold values from 0.1 to 1
- interior_power_source: float32 [512, 256, 128], P('lon', 'lat'), may hold values from -6 to 6
- earlier_east_west_basis: float32 [512, 32], P('lon'), may hold values from -0.25 to 0.25
- earlier_north_south_basis: float32 [256, 32], P('lat'), may hold values from -0.375 to 0.375
- earlier_depthwise_basis: float32 [128, 32], replicated, may hold values from -0.5 to 0.5
Outputs:
- final_kelvin_map: float32 [512, 256, 128], P('lon', 'lat')
- error: float32 [512, 256, 128], P('lon', 'lat')
- new_lon: float32 [512, 32], P('lon')
- new_lat: float32 [256, 32], P('lat')
- new_rad: float32 [128, 32], replicated
- core: float32 [32, 32, 32], replicated
The draws below stay inside these ranges and needn't reach their ends.
All inputs are finite; a program needn't handle non-finite values.
Results may differ from the reference program's by a relative error of at most 0.02.
Values sent between devices are 32-bit elements; how exact they have to be, the bound alone decides.
A program may use at most 64 MiB of HBM per device.

```python
import math
import jax
import jax.numpy as jnp
from jax import lax

SHELL_LAYERS = 128
R = 32
STEPS = 4
EAST_WEST_SIZE = 512
NORTH_SOUTH_SIZE = 256


def block_scale(key, dims, split, least, top_value):
    loudness, own = 1.0, jax.random.fold_in(key, 6)
    for dim, parts in split:
        steps = jnp.exp(jax.random.uniform(jax.random.fold_in(own, dim), (parts,), jnp.float32, least / len(split), top_value / len(split)))
        loudness = loudness * jnp.repeat(steps, dims[dim] // parts).reshape([-1 if axis == dim else 1 for axis in range(len(dims))])
    return loudness


def centred(key, shape, scale, limit, split=(), dtype=jnp.bfloat16):
    entries = scale * jax.random.normal(key, shape, jnp.float32)
    if split:
        entries = entries * block_scale(key, shape, split, -0.22, 0.18)
    return jnp.clip(entries, -limit, limit).astype(dtype)


def setup_inputs(seed: int = 0) -> dict:
    key_list = jax.random.split(jax.random.key(seed), 7)
    return {
        "initial_kelvin_map": centred(key_list[0], (EAST_WEST_SIZE, NORTH_SOUTH_SIZE, SHELL_LAYERS), 1.0, 6.0, ((0, 8), (1, 4)), jnp.float32),
        "thermal_diffusivity_map": jnp.clip(jnp.exp(math.log(1.0) - 2.3025851 * jax.random.uniform(key_list[1], (EAST_WEST_SIZE, NORTH_SOUTH_SIZE, SHELL_LAYERS), jnp.float32) ** block_scale(key_list[1], (EAST_WEST_SIZE, NORTH_SOUTH_SIZE, SHELL_LAYERS), ((0, 8), (1, 4)), -0.2, 0.2)), 0.1, 1.0),
        "interior_power_source": centred(key_list[2], (EAST_WEST_SIZE, NORTH_SOUTH_SIZE, SHELL_LAYERS), 1.0, 6.0, ((0, 8), (1, 4)), jnp.float32),
        "earlier_east_west_basis": centred(key_list[3], (EAST_WEST_SIZE, R), EAST_WEST_SIZE ** -0.5, 0.25, ((0, 8),), jnp.float32),
        "earlier_north_south_basis": centred(key_list[4], (NORTH_SOUTH_SIZE, R), NORTH_SOUTH_SIZE ** -0.5, 0.375, ((0, 4),), jnp.float32),
        "earlier_depthwise_basis": centred(key_list[5], (SHELL_LAYERS, R), SHELL_LAYERS ** -0.5, 0.5, (), jnp.float32),
    }


highest = lax.Precision.HIGHEST
time_step = 0.15

def harmonic(cond_a, cond_b):
    summed = cond_a + cond_b
    return 2.0 * cond_a * cond_b / jnp.where(summed > 0.0, summed, 1.0)

def advance(padded, cond_pad, interior_power_source):
    centre = padded[1:-1, 1:-1]
    kcentre = cond_pad[1:-1, 1:-1]
    change = interior_power_source
    pairs = ((padded[2:, 1:-1], cond_pad[2:, 1:-1]), (padded[:-2, 1:-1], cond_pad[:-2, 1:-1]), (padded[1:-1, 2:], cond_pad[1:-1, 2:]), (padded[1:-1, :-2], cond_pad[1:-1, :-2]))
    for near_t, near_k in pairs:
        change = change + harmonic(kcentre, near_k) * (near_t - centre)
    radial_t = jnp.pad(centre, ((0, 0), (0, 0), (1, 1)))
    radial_k = jnp.pad(kcentre, ((0, 0), (0, 0), (1, 1)))
    change = change + harmonic(kcentre, radial_k[:, :, 2:]) * (radial_t[:, :, 2:] - centre)
    change = change + harmonic(kcentre, radial_k[:, :, :-2]) * (radial_t[:, :, :-2] - centre)
    return centre + time_step * change

def extend(values):
    wrapped = jnp.pad(values, ((1, 1), (0, 0), (0, 0)), mode='wrap')
    return jnp.pad(wrapped, ((0, 0), (1, 1), (0, 0)))

def orthonormal(block, gram):
    factor_l = jnp.linalg.cholesky(gram)
    return lax.linalg.triangular_solve(factor_l, block, left_side=False, lower=True, transpose_a=True)

def refine(modes, factor):
    proj = jnp.dot(modes.T, factor, precision=highest)
    block = jnp.dot(modes, proj, precision=highest)
    gram = jnp.dot(block.T, block, precision=highest)
    return orthonormal(block, gram)

def reference(initial_kelvin_map, thermal_diffusivity_map, interior_power_source, earlier_east_west_basis, earlier_north_south_basis, earlier_depthwise_basis):
    cond_pad = extend(thermal_diffusivity_map)
    final_kelvin_map = initial_kelvin_map
    for step_index in range(STEPS):
        final_kelvin_map = advance(extend(final_kelvin_map), cond_pad, interior_power_source)
    rad_proj = jnp.dot(final_kelvin_map.reshape(EAST_WEST_SIZE * NORTH_SOUTH_SIZE, SHELL_LAYERS), earlier_depthwise_basis, precision=highest).reshape(EAST_WEST_SIZE, NORTH_SOUTH_SIZE, R)
    modes = jnp.einsum('ijb,ja->iab', rad_proj, earlier_north_south_basis, precision=highest).reshape(EAST_WEST_SIZE, R * R)
    new_lon = refine(modes, earlier_east_west_basis)
    modes = jnp.einsum('ijb,ia->jab', rad_proj, new_lon, precision=highest).reshape(NORTH_SOUTH_SIZE, R * R)
    new_lat = refine(modes, earlier_north_south_basis)
    lon_proj = jnp.dot(new_lon.T, final_kelvin_map.reshape(EAST_WEST_SIZE, NORTH_SOUTH_SIZE * SHELL_LAYERS), precision=highest).reshape(R, NORTH_SOUTH_SIZE, SHELL_LAYERS)
    modes = jnp.einsum('ajr,jb->rab', lon_proj, new_lat, precision=highest).reshape(SHELL_LAYERS, R * R)
    new_rad = refine(modes, earlier_depthwise_basis)
    core = jnp.einsum('rab,rc->abc', modes.reshape(SHELL_LAYERS, R, R), new_rad, precision=highest)
    first = jnp.einsum('abc,rc->abr', core, new_rad, precision=highest)
    second = jnp.einsum('abr,jb->ajr', first, new_lat, precision=highest)
    recon = jnp.dot(new_lon, second.reshape(R, NORTH_SOUTH_SIZE * SHELL_LAYERS), precision=highest).reshape(EAST_WEST_SIZE, NORTH_SOUTH_SIZE, SHELL_LAYERS)
    return (final_kelvin_map, final_kelvin_map - recon, new_lon, new_lat, new_rad, core)
```

```python
import functools

import jax
import jax.numpy as jnp
from jax import lax
from jax.experimental import pallas as pl
from jax.experimental.pallas import tpu as pltpu
from jax.sharding import PartitionSpec as P

STEPS = 4
time_step = 0.15
F32 = jnp.float32
BF16 = jnp.bfloat16
NN = (((1,), (0,)), ((), ()))
NT = (((1,), (1,)), ((), ()))
TN = (((0,), (0,)), ((), ()))


def split(x):
    hi = x.astype(BF16)
    return hi, (x - hi.astype(F32)).astype(BF16)


def dot3(a, b, dims=NN):
    ah, al = a
    bh, bl = b
    d = functools.partial(lax.dot_general, dimension_numbers=dims, preferred_element_type=F32)
    return d(ah, bh) + d(ah, bl) + d(al, bh)


def mm(a, b, dims=NN):
    return dot3(split(a), split(b), dims)


def mmh(a, b, dims=NN):
    return lax.dot_general(
        a, b, dims, precision=lax.Precision.HIGHEST, preferred_element_type=F32
    )


def chol_inverse(gram):
    n = gram.shape[0]
    row = lax.broadcasted_iota(jnp.int32, (n, n), 0)
    col = lax.broadcasted_iota(jnp.int32, (n, n), 1)
    eye = jnp.where(row == col, 1.0, 0.0).astype(F32)
    m = jnp.concatenate([gram, eye], axis=1)
    rows = lax.broadcasted_iota(jnp.int32, (n, 1), 0)
    for k in range(n - 1):
        top = m[k : k + 1, :]
        factor = jnp.where(rows > k, m[:, k : k + 1] / m[k : k + 1, k : k + 1], 0.0)
        m = m - factor * top
    diag = jnp.sum(jnp.where(row == col, m[:, :n], 0.0), axis=1, keepdims=True)
    return m[:, n:] / jnp.sqrt(diag)


def block_diag(x, count):
    n = x.shape[0]
    wide = jnp.concatenate([x] * count, axis=1)
    full = jnp.concatenate([wide] * count, axis=0)
    row = lax.broadcasted_iota(jnp.int32, full.shape, 0) // n
    col = lax.broadcasted_iota(jnp.int32, full.shape, 1) // n
    return jnp.where(row == col, full, 0.0)


class Comm:
    def __init__(self, nl, nz, send_sem, recv_sem):
        self.nl, self.nz = nl, nz
        self.lon = lax.axis_index("lon")
        self.lat = lax.axis_index("lat")
        self.send_sem, self.recv_sem = send_sem, recv_sem
        self.phase = 0
        self.sent = []

    def start(self, axis, source, target):
        count = self.nl if axis == "lon" else self.nz
        me = self.lon if axis == "lon" else self.lat
        ph = self.phase
        self.phase += 1
        waits = []
        for d in range(1, count):
            peer = lax.rem(me + d, count)
            owner = lax.rem(me + count - d, count)
            copy = pltpu.make_async_remote_copy(
                src_ref=source(peer),
                dst_ref=target(me),
                send_sem=self.send_sem.at[ph, d],
                recv_sem=self.recv_sem.at[ph, d],
                device_id={axis: peer},
                device_id_type=pl.DeviceIdType.MESH,
            )
            copy.start()
            self.sent.append(copy)
            waits.append(
                pltpu.make_async_remote_copy(
                    src_ref=target(owner),
                    dst_ref=target(owner),
                    send_sem=self.send_sem.at[ph, d],
                    recv_sem=self.recv_sem.at[ph, d],
                    device_id={axis: peer},
                    device_id_type=pl.DeviceIdType.MESH,
                )
            )
        return waits

    def gather(self, axis, slots):
        me = self.lon if axis == "lon" else self.lat
        return self.start(axis, lambda peer: slots.at[me], lambda owner: slots.at[owner])

    def wait(self, waits):
        for w in waits:
            w.wait_recv()

    def finish(self):
        for c in self.sent:
            c.wait_send()


def total(slots):
    out = slots[0]
    for k in range(1, slots.shape[0]):
        out = out + slots[k]
    return out


def all_reduce(comm, buf, rs, zs, ag, during=None):
    rows = rs.shape[1]
    piece = lambda ref, p: ref.at[pl.ds(pl.multiple_of(p * rows, rows), rows)]
    first = comm.start("lon", lambda peer: piece(buf, peer), lambda owner: rs.at[owner])
    rs[comm.lon] = piece(buf, comm.lon)[...]
    if during is not None:
        during[0]()
    comm.wait(first)
    zs[comm.lat] = total(rs)
    second = comm.gather("lat", zs)
    if during is not None:
        during[1]()
    comm.wait(second)
    piece(ag, comm.lon)[...] = total(zs)
    third = comm.start("lon", lambda peer: piece(ag, comm.lon), lambda owner: piece(ag, owner))
    if during is not None:
        during[2]()
    comm.wait(third)


def sweep_kernel(nl, nz, t_ref, u_ref, v_ref, w_ref,
                 err_ref, lon_ref, lat_ref, rad_ref, core_ref,
                 z1, x3, y3, f_ref, y1, y2, small,
                 b1s, b2s, b3l, b3z, g1s, g2s, bufs, rss, zss, ags,
                 send_sem, recv_sem):
    comm = Comm(nl, nz, send_sem, recv_sem)
    ni, nj, nr = t_ref.shape
    r = u_ref.shape[1]
    group = 128 // r
    blocks = r // group

    barrier = pltpu.get_barrier_semaphore()
    for d in range(1, nl):
        pl.semaphore_signal(barrier, inc=1, device_id={"lon": lax.rem(comm.lon + d, nl)},
                            device_id_type=pl.DeviceIdType.MESH)
    for d in range(1, nz):
        pl.semaphore_signal(barrier, inc=1, device_id={"lat": lax.rem(comm.lat + d, nz)},
                            device_id_type=pl.DeviceIdType.MESH)

    wt = w_ref[...].T
    wts = split(wt)
    ut = u_ref[...].T
    vt = v_ref[...].T

    @pl.loop(0, ni // 8)
    def _(step):
        for k in range(8):
            i = step * 8 + k
            z1[:, i, :] = dot3(wts, split(t_ref[i]), NT)

    lane = lambda n: lax.broadcasted_iota(jnp.int32, (n, 128), 1) // r
    v4 = split(jnp.concatenate([v_ref[...]] * group, axis=1))
    uts = split(ut)
    for m in range(blocks):
        out = jnp.zeros((ni, 128), F32)
        for g in range(group):
            out = jnp.where(lane(ni) == g, dot3(split(z1[m * group + g]), v4), out)
        y1[m] = out
        bufs[0, pl.ds(m * r, r), :] = dot3(uts, split(out))

    pl.semaphore_wait(barrier, nl + nz - 2)

    all_reduce(comm, bufs.at[0], rss.at[0], zss.at[0], ags.at[0])

    acc = jnp.zeros((r, ni), F32)
    for m in range(blocks):
        acc = acc + mm(ags[0, pl.ds(m * r, r), :], y1[m], NT)
    b1s[comm.lat] = acc
    w = comm.gather("lat", b1s)
    comm.wait(w)
    b1t = total(b1s)
    g1s[comm.lon] = mmh(b1t, b1t, NT)
    g1w = comm.gather("lon", g1s)
    b1x = split(jnp.concatenate([b1t] * group, axis=0).T)
    vts = split(vt)
    for m in range(blocks):
        out = jnp.zeros((nj, 128), F32)
        for g in range(group):
            out = jnp.where(lane(nj) == g, dot3(split(z1[m * group + g]), b1x, TN), out)
        y2[m] = out
        bufs[1, pl.ds(m * r, r), :] = dot3(vts, split(out))

    def chol1():
        comm.wait(g1w)
        small[0] = chol_inverse(total(g1s))

    nothing = lambda: None
    all_reduce(comm, bufs.at[1], rss.at[1], zss.at[1], ags.at[1], (nothing, chol1, nothing))

    l1 = small[0]
    bd1 = split(block_diag(mmh(l1, l1, TN), group))
    acc = jnp.zeros((r, nj), F32)
    for m in range(blocks):
        acc = acc + mm(dot3(split(ags[1, pl.ds(m * r, r), :]), bd1), y2[m], NT)
    b2s[comm.lon] = acc
    w = comm.gather("lon", b2s)
    lont = mmh(l1, b1t)
    lon_ref[...] = lont.T
    comm.wait(w)
    b2t = total(b2s)
    g2s[comm.lat] = mmh(b2t, b2t, NT)
    g2w = comm.gather("lat", g2s)
    b2h = split(b2t)

    @pl.loop(0, ni // 8)
    def _(step):
        for k in range(8):
            i = step * 8 + k
            x3[i] = dot3(b2h, split(t_ref[i]))

    lonh = split(lont)
    for b in range(r):
        y3[:, b, :] = dot3(lonh, split(x3[:, b, :]))

    per = 128 // r

    def y3block(m):
        return split(y3[pl.ds(m * per, per)].reshape(128, nr))

    for m in range(blocks):
        bufs[2, pl.ds(m * r, r), :] = dot3(wts, y3block(m), NT)

    def chol2():
        comm.wait(g2w)
        small[1] = chol_inverse(total(g2s))

    all_reduce(comm, bufs.at[2], rss.at[2], zss.at[2], ags.at[2], (chol2, nothing, nothing))

    l2 = small[1]
    bd2 = split(block_diag(mmh(l2, l2, TN), group))
    acc = jnp.zeros((r, nr), F32)
    for m in range(blocks):
        acc = acc + dot3(split(dot3(split(ags[2, pl.ds(m * r, r), :]), bd2)), y3block(m))
    b3l[comm.lon] = acc
    w = comm.gather("lon", b3l)
    latt = mmh(l2, b2t)
    lat_ref[...] = latt.T
    comm.wait(w)
    b3z[comm.lat] = total(b3l)
    w = comm.gather("lat", b3z)
    comm.wait(w)
    b3t = total(b3z)
    l3 = chol_inverse(mmh(b3t, b3t, NT))
    radt = mmh(l3, b3t)
    rad_ref[...] = radt.T
    radh = split(radt)
    for m in range(blocks):
        bufs[3, pl.ds(m * r, r), :] = dot3(radh, y3block(m), NT)
    all_reduce(comm, bufs.at[3], rss.at[3], zss.at[3], ags.at[3])

    bdl = split(block_diag(l2.T, group))
    for m in range(blocks):
        core = dot3(split(ags[3, pl.ds(m * r, r), :]), bdl)
        core_ref[pl.ds(m * 128, 128), :] = core.T
        f_ref[pl.ds(m * per, per)] = dot3(split(core), radh, TN).reshape(per, r, nr)
    lonb = split(lon_ref[...])
    latb = split(lat_ref[...])
    for b in range(r):
        x3[:, b, :] = dot3(lonb, split(f_ref[:, b, :]))

    @pl.loop(0, ni // 8)
    def _(step):
        for k in range(8):
            i = step * 8 + k
            err_ref[i] = t_ref[i] - dot3(latb, split(x3[i]))

    comm.finish()


def sweep(t, u, v, w):
    nl, nz = lax.axis_size("lon"), lax.axis_size("lat")
    ni, nj, nr = t.shape
    r = u.shape[1]
    rows = r * r * r // 128
    piece = rows // nl
    blocks = r * r // 128
    most = max(nl, nz)
    vm = pl.BlockSpec(memory_space=pltpu.VMEM)
    sds = lambda *s: jax.ShapeDtypeStruct(s, F32)
    V = lambda *s: pltpu.VMEM(s, F32)
    phases = 18
    err, lon, lat, rad, core = pl.pallas_call(
        functools.partial(sweep_kernel, nl, nz),
        out_shape=(sds(ni, nj, nr), sds(ni, r), sds(nj, r), sds(nr, r), sds(r * r, r)),
        in_specs=[vm] * 4,
        out_specs=(vm,) * 5,
        scratch_shapes=[
            V(r, ni, nj), V(ni, r, nr), V(r, r, nr), V(r, r, nr),
            V(blocks, ni, 128), V(blocks, nj, 128), V(2, r, r),
            V(nz, r, ni), V(nl, r, nj), V(nl, r, nr), V(nz, r, nr),
            V(nl, r, r), V(nz, r, r),
            V(4, rows, 128), V(4, nl, piece, 128), V(4, nz, piece, 128), V(4, rows, 128),
            pltpu.SemaphoreType.DMA((phases, most)),
            pltpu.SemaphoreType.DMA((phases, most)),
        ],
        compiler_params=pltpu.CompilerParams(
            collective_id=1, has_side_effects=True, vmem_limit_bytes=40 * 1024 * 1024
        ),
    )(t, u, v, w)
    return err, lon, lat, rad, core.reshape(r, r, r)


def extended(x, sides, width, wrap):
    for axis, dim in sides:
        count, length = (lax.axis_size(axis), x.shape[dim])
        up = [(i, (i + 1) % count) for i in range(count if wrap else count - 1)]
        down = [(j, i) for i, j in up]
        last = lax.slice_in_dim(x, length - width, length, axis=dim)
        initial = lax.slice_in_dim(x, 0, width, axis=dim)
        before = lax.ppermute(last, axis, up)
        after = lax.ppermute(initial, axis, down)
        x = jnp.concatenate([before, x, after], axis=dim)
    return x


def harmonic(cond_a, cond_b):
    summed = cond_a + cond_b
    return 2.0 * cond_a * cond_b / jnp.where(summed > 0.0, summed, 1.0)


def advance(padded, cond_pad, interior_power_source):
    centre = padded[1:-1, 1:-1]
    kcentre = cond_pad[1:-1, 1:-1]
    change = interior_power_source
    pairs = (
        (padded[2:, 1:-1], cond_pad[2:, 1:-1]),
        (padded[:-2, 1:-1], cond_pad[:-2, 1:-1]),
        (padded[1:-1, 2:], cond_pad[1:-1, 2:]),
        (padded[1:-1, :-2], cond_pad[1:-1, :-2]),
    )
    for near_t, near_k in pairs:
        change = change + harmonic(kcentre, near_k) * (near_t - centre)
    radial_t = jnp.pad(centre, ((0, 0), (0, 0), (1, 1)))
    radial_k = jnp.pad(kcentre, ((0, 0), (0, 0), (1, 1)))
    change = change + harmonic(kcentre, radial_k[:, :, 2:]) * (radial_t[:, :, 2:] - centre)
    change = change + harmonic(kcentre, radial_k[:, :, :-2]) * (radial_t[:, :, :-2] - centre)
    return centre + time_step * change


def local(temp, cond, source, lon_basis, lat_basis, rad_basis):
    cond_lon = extended(cond, (("lon", 0),), 1, True)
    cond_pad = extended(cond_lon, (("lat", 1),), 1, False)
    for _ in range(STEPS):
        temp_lon = extended(temp, (("lon", 0),), 1, True)
        padded = extended(temp_lon, (("lat", 1),), 1, False)
        temp = advance(padded, cond_pad, source)
    err, lon, lat, rad, core = sweep(temp, lon_basis, lat_basis, rad_basis)
    return temp, err, lon, lat, rad, core


def solution(mesh):
    grid = P("lon", "lat", None)
    in_specs = (grid, grid, grid, P("lon", None), P("lat", None), P())
    out_specs = (grid, grid, P("lon", None), P("lat", None), P(), P())
    return jax.shard_map(local, mesh=mesh, in_specs=in_specs, out_specs=out_specs, check_vma=False)
```

```python
import functools

import jax
import jax.numpy as jnp
from jax import lax
from jax.experimental import pallas as pl
from jax.experimental.pallas import tpu as pltpu
from jax.sharding import PartitionSpec as P

STEPS = 4
time_step = 0.15
F32 = jnp.float32
BF16 = jnp.bfloat16
NN = (((1,), (0,)), ((), ()))
NT = (((1,), (1,)), ((), ()))
TN = (((0,), (0,)), ((), ()))


def split(x):
    hi = x.astype(BF16)
    return hi, (x - hi.astype(F32)).astype(BF16)


def dot3(a, b, dims=NN):
    ah, al = a
    bh, bl = b
    d = functools.partial(lax.dot_general, dimension_numbers=dims, preferred_element_type=F32)
    return d(ah, bh) + d(ah, bl) + d(al, bh)


def mm(a, b, dims=NN):
    return dot3(split(a), split(b), dims)


def mmh(a, b, dims=NN):
    return lax.dot_general(
        a, b, dims, precision=lax.Precision.HIGHEST, preferred_element_type=F32
    )


def chol_inverse(gram):
    n = gram.shape[0]
    row = lax.broadcasted_iota(jnp.int32, (n, n), 0)
    col = lax.broadcasted_iota(jnp.int32, (n, n), 1)
    eye = jnp.where(row == col, 1.0, 0.0).astype(F32)
    m = jnp.concatenate([gram, eye], axis=1)
    rows = lax.broadcasted_iota(jnp.int32, (n, 1), 0)
    for k in range(n - 1):
        top = m[k : k + 1, :]
        factor = jnp.where(rows > k, m[:, k : k + 1] / m[k : k + 1, k : k + 1], 0.0)
        m = m - factor * top
    diag = jnp.sum(jnp.where(row == col, m[:, :n], 0.0), axis=1, keepdims=True)
    return m[:, n:] / jnp.sqrt(diag)


def block_diag(x, count):
    n = x.shape[0]
    wide = jnp.concatenate([x] * count, axis=1)
    full = jnp.concatenate([wide] * count, axis=0)
    row = lax.broadcasted_iota(jnp.int32, full.shape, 0) // n
    col = lax.broadcasted_iota(jnp.int32, full.shape, 1) // n
    return jnp.where(row == col, full, 0.0)


class Comm:
    def __init__(self, nl, nz, send_sem, recv_sem, halo_send, halo_recv):
        self.halo_send, self.halo_recv = halo_send, halo_recv
        self.nl, self.nz = nl, nz
        self.lon = lax.axis_index("lon")
        self.lat = lax.axis_index("lat")
        self.send_sem, self.recv_sem = send_sem, recv_sem
        self.phase = 0
        self.sent = []

    def start(self, axis, source, target):
        count = self.nl if axis == "lon" else self.nz
        me = self.lon if axis == "lon" else self.lat
        ph = self.phase
        self.phase += 1
        waits = []
        for d in range(1, count):
            peer = lax.rem(me + d, count)
            owner = lax.rem(me + count - d, count)
            copy = pltpu.make_async_remote_copy(
                src_ref=source(peer),
                dst_ref=target(me),
                send_sem=self.send_sem.at[ph, d],
                recv_sem=self.recv_sem.at[ph, d],
                device_id={axis: peer},
                device_id_type=pl.DeviceIdType.MESH,
            )
            copy.start()
            self.sent.append(copy)
            waits.append(
                pltpu.make_async_remote_copy(
                    src_ref=target(owner),
                    dst_ref=target(owner),
                    send_sem=self.send_sem.at[ph, d],
                    recv_sem=self.recv_sem.at[ph, d],
                    device_id={axis: peer},
                    device_id_type=pl.DeviceIdType.MESH,
                )
            )
        return waits

    def send(self, axis, shift, k, lane, source, target):
        count = self.nl if axis == "lon" else self.nz
        me = self.lon if axis == "lon" else self.lat
        return pltpu.make_async_remote_copy(
            src_ref=source,
            dst_ref=target,
            send_sem=self.halo_send.at[k, lane],
            recv_sem=self.halo_recv.at[k, lane],
            device_id={axis: lax.rem(me + shift + count, count)},
            device_id_type=pl.DeviceIdType.MESH,
        )

    def gather(self, axis, slots):
        me = self.lon if axis == "lon" else self.lat
        return self.start(axis, lambda peer: slots.at[me], lambda owner: slots.at[owner])

    def wait(self, waits):
        for w in waits:
            w.wait_recv()

    def finish(self):
        for c in self.sent:
            c.wait_send()


def total(slots):
    out = slots[0]
    for k in range(1, slots.shape[0]):
        out = out + slots[k]
    return out


def all_reduce(comm, buf, rs, zs, ag, during=None):
    rows = rs.shape[1]
    piece = lambda ref, p: ref.at[pl.ds(pl.multiple_of(p * rows, rows), rows)]
    first = comm.start("lon", lambda peer: piece(buf, peer), lambda owner: rs.at[owner])
    rs[comm.lon] = piece(buf, comm.lon)[...]
    if during is not None:
        during[0]()
    comm.wait(first)
    zs[comm.lat] = total(rs)
    second = comm.gather("lat", zs)
    if during is not None:
        during[1]()
    comm.wait(second)
    piece(ag, comm.lon)[...] = total(zs)
    third = comm.start("lon", lambda peer: piece(ag, comm.lon), lambda owner: piece(ag, owner))
    if during is not None:
        during[2]()
    comm.wait(third)


def harmonic(cond_a, cond_b):
    summed = cond_a + cond_b
    return 2.0 * cond_a * cond_b / jnp.where(summed > 0.0, summed, 1.0)


def conduct(comm, t0, k_ref, q_ref, tb, hx, hy, hz, edge_k, hal_lon, hal_lat, pack):
    ni, nj, nr = t0.shape
    last_step = STEPS
    has_lo, has_hi = comm.lat > 0, comm.lat < comm.nz - 1

    def exchange(k, src):
        lon_copies = (
            comm.send("lon", 1, k, 0, src.at[ni - 1], hal_lon.at[k, 0]),
            comm.send("lon", -1, k, 1, src.at[0], hal_lon.at[k, 1]),
        )
        lat_copies = (
            (has_hi, has_lo, comm.send("lat", 1, k, 2, pack.at[k, 1], hal_lat.at[k, 0])),
            (has_lo, has_hi, comm.send("lat", -1, k, 3, pack.at[k, 0], hal_lat.at[k, 1])),
        )
        for c in lon_copies:
            c.start()
        for out, _, c in lat_copies:
            pl.when(out)(c.start)

        def wait():
            for c in lon_copies:
                c.wait_recv()
            for _, into, c in lat_copies:
                pl.when(into)(c.wait_recv)

        def wait_sent():
            for c in lon_copies:
                c.wait_send()
            for out, _, c in lat_copies:
                pl.when(out)(c.wait_send)

        return wait, wait_sent

    @pl.when(comm.lat == 0)
    def _():
        for k in range(STEPS + 1):
            hal_lat[k, 0] = jnp.zeros((ni, nr), F32)

    @pl.when(comm.lat == comm.nz - 1)
    def _():
        for k in range(STEPS + 1):
            hal_lat[k, 1] = jnp.zeros((ni, nr), F32)

    pack[last_step, 0] = k_ref[:, 0, :]
    pack[last_step, 1] = k_ref[:, nj - 1, :]
    pack[0, 0] = t0[:, 0, :]
    pack[0, 1] = t0[:, nj - 1, :]
    wait_k, sent_k = exchange(last_step, k_ref)
    wait_t, sent_t = exchange(0, t0)

    row = lax.broadcasted_iota(jnp.int32, (nj, nr), 0)
    col = lax.broadcasted_iota(jnp.int32, (nj, nr), 1)

    def faces(i):
        k = k_ref[i]
        hy[i] = jnp.where(row == 0, 0.0, harmonic(k, pltpu.roll(k, 1, 0)))
        hz[i] = jnp.where(col == 0, 0.0, harmonic(k, pltpu.roll(k, 1, 1)))

    @pl.loop(1, ni)
    def _(i):
        faces(i)
        hx[i] = harmonic(k_ref[i], k_ref[i - 1])

    faces(0)
    wait_k()
    hx[0] = harmonic(k_ref[0], hal_lon[last_step, 0])
    hx[ni] = harmonic(k_ref[ni - 1], hal_lon[last_step, 1])
    edge_k[0] = harmonic(pack[last_step, 0], hal_lat[last_step, 0])
    edge_k[1] = harmonic(pack[last_step, 1], hal_lat[last_step, 1])

    def slab(i, before, here, after):
        fx = hx[i + 1] * (after - here) - hx[i] * (here - before)
        fy = hy[i] * (here - pltpu.roll(here, 1, 0))
        fz = hz[i] * (here - pltpu.roll(here, 1, 1))
        change = q_ref[i] + fx + (pltpu.roll(fy, nj - 1, 0) - fy) + (pltpu.roll(fz, nr - 1, 1) - fz)
        return here + time_step * change

    for step in range(STEPS):
        src = t0 if step == 0 else tb.at[(step - 1) % 2]
        dst = tb.at[step % 2]

        @pl.loop(1, ni - 1)
        def _(i):
            dst[i] = slab(i, src[i - 1], src[i], src[i + 1])

        wait_t()
        dst[0] = slab(0, hal_lon[step, 0], src[0], src[1])
        dst[ni - 1] = slab(ni - 1, src[ni - 2], src[ni - 1], hal_lon[step, 1])
        for side, j in ((0, 0), (1, nj - 1)):
            flux = edge_k[side] * (hal_lat[step, side] - pack[step, side])
            edge = dst[:, j, :] + time_step * flux
            dst[:, j, :] = edge
            if step < STEPS - 1:
                pack[step + 1, side] = edge
        sent_t()
        if step < STEPS - 1:
            wait_t, sent_t = exchange(step + 1, dst)
    sent_k()


def sweep_kernel(nl, nz, t0, k_ref, q_ref, u_ref, v_ref, w_ref,
                 temp_ref, x3, lon_ref, lat_ref, rad_ref, core_ref,
                 tb, hx, hy, hz, edge_k, hal_lon, hal_lat, pack,
                 z1, y3, f_ref, y1, y2, small,
                 b1s, b2s, b3l, b3z, g1s, g2s, bufs, rss, zss, ags,
                 send_sem, recv_sem, halo_send, halo_recv, out_sem):
    comm = Comm(nl, nz, send_sem, recv_sem, halo_send, halo_recv)
    ni, nj, nr = t0.shape
    t_ref = tb.at[(STEPS - 1) % 2]
    r = u_ref.shape[1]
    group = 128 // r
    blocks = r // group

    barrier = pltpu.get_barrier_semaphore()
    for d in range(1, nl):
        pl.semaphore_signal(barrier, inc=1, device_id={"lon": lax.rem(comm.lon + d, nl)},
                            device_id_type=pl.DeviceIdType.MESH)
    for d in range(1, nz):
        pl.semaphore_signal(barrier, inc=1, device_id={"lat": lax.rem(comm.lat + d, nz)},
                            device_id_type=pl.DeviceIdType.MESH)

    pl.semaphore_wait(barrier, nl + nz - 2)
    conduct(comm, t0, k_ref, q_ref, tb, hx, hy, hz, edge_k, hal_lon, hal_lat, pack)
    out_copy = pltpu.make_async_copy(t_ref, temp_ref, out_sem)
    out_copy.start()

    wt = w_ref[...].T
    wts = split(wt)
    ut = u_ref[...].T
    vt = v_ref[...].T

    @pl.loop(0, ni // 8)
    def _(step):
        for k in range(8):
            i = step * 8 + k
            z1[:, i, :] = dot3(wts, split(t_ref[i]), NT)

    lane = lambda n: lax.broadcasted_iota(jnp.int32, (n, 128), 1) // r
    v4 = split(jnp.concatenate([v_ref[...]] * group, axis=1))
    uts = split(ut)
    for m in range(blocks):
        out = jnp.zeros((ni, 128), F32)
        for g in range(group):
            out = jnp.where(lane(ni) == g, dot3(split(z1[m * group + g]), v4), out)
        y1[m] = out
        bufs[0, pl.ds(m * r, r), :] = dot3(uts, split(out))

    all_reduce(comm, bufs.at[0], rss.at[0], zss.at[0], ags.at[0])

    acc = jnp.zeros((r, ni), F32)
    for m in range(blocks):
        acc = acc + mm(ags[0, pl.ds(m * r, r), :], y1[m], NT)
    b1s[comm.lat] = acc
    w = comm.gather("lat", b1s)
    comm.wait(w)
    b1t = total(b1s)
    g1s[comm.lon] = mmh(b1t, b1t, NT)
    g1w = comm.gather("lon", g1s)
    b1x = split(jnp.concatenate([b1t] * group, axis=0).T)
    vts = split(vt)
    for m in range(blocks):
        out = jnp.zeros((nj, 128), F32)
        for g in range(group):
            out = jnp.where(lane(nj) == g, dot3(split(z1[m * group + g]), b1x, TN), out)
        y2[m] = out
        bufs[1, pl.ds(m * r, r), :] = dot3(vts, split(out))

    def chol1():
        comm.wait(g1w)
        small[0] = chol_inverse(total(g1s))

    nothing = lambda: None
    all_reduce(comm, bufs.at[1], rss.at[1], zss.at[1], ags.at[1], (nothing, chol1, nothing))

    l1 = small[0]
    bd1 = split(block_diag(mmh(l1, l1, TN), group))
    acc = jnp.zeros((r, nj), F32)
    for m in range(blocks):
        acc = acc + mm(dot3(split(ags[1, pl.ds(m * r, r), :]), bd1), y2[m], NT)
    b2s[comm.lon] = acc
    w = comm.gather("lon", b2s)
    lont = mmh(l1, b1t)
    lon_ref[...] = lont.T
    comm.wait(w)
    b2t = total(b2s)
    g2s[comm.lat] = mmh(b2t, b2t, NT)
    g2w = comm.gather("lat", g2s)
    b2h = split(b2t)

    @pl.loop(0, ni // 8)
    def _(step):
        for k in range(8):
            i = step * 8 + k
            x3[i] = dot3(b2h, split(t_ref[i]))

    lonh = split(lont)
    for b in range(r):
        y3[:, b, :] = dot3(lonh, split(x3[:, b, :]))

    per = 128 // r

    def y3block(m):
        return split(y3[pl.ds(m * per, per)].reshape(128, nr))

    for m in range(blocks):
        bufs[2, pl.ds(m * r, r), :] = dot3(wts, y3block(m), NT)

    def chol2():
        comm.wait(g2w)
        small[1] = chol_inverse(total(g2s))

    all_reduce(comm, bufs.at[2], rss.at[2], zss.at[2], ags.at[2], (chol2, nothing, nothing))

    l2 = small[1]
    bd2 = split(block_diag(mmh(l2, l2, TN), group))
    acc = jnp.zeros((r, nr), F32)
    for m in range(blocks):
        acc = acc + dot3(split(dot3(split(ags[2, pl.ds(m * r, r), :]), bd2)), y3block(m))
    b3l[comm.lon] = acc
    w = comm.gather("lon", b3l)
    latt = mmh(l2, b2t)
    lat_ref[...] = latt.T
    comm.wait(w)
    b3z[comm.lat] = total(b3l)
    w = comm.gather("lat", b3z)
    comm.wait(w)
    b3t = total(b3z)
    l3 = chol_inverse(mmh(b3t, b3t, NT))
    radt = mmh(l3, b3t)
    rad_ref[...] = radt.T
    radh = split(radt)
    for m in range(blocks):
        bufs[3, pl.ds(m * r, r), :] = dot3(radh, y3block(m), NT)
    all_reduce(comm, bufs.at[3], rss.at[3], zss.at[3], ags.at[3])

    bdl = split(block_diag(l2.T, group))
    for m in range(blocks):
        core = dot3(split(ags[3, pl.ds(m * r, r), :]), bdl)
        core_ref[pl.ds(m * 128, 128), :] = core.T
        f_ref[pl.ds(m * per, per)] = dot3(split(core), radh, TN).reshape(per, r, nr)
    lonb = split(lon_ref[...])
    for b in range(r):
        x3[:, b, :] = dot3(lonb, split(f_ref[:, b, :]))
    out_copy.wait()
    comm.finish()


def error_kernel(t_ref, s_ref, lon_ref, lat_ref, rad_ref, core_ref,
                 temp_out, err_out, lon_out, lat_out, rad_out, core_out):
    latb = split(lat_ref[...])
    for i in range(t_ref.shape[0]):
        err_out[i] = t_ref[i] - dot3(latb, split(s_ref[i]))
    temp_out[...] = t_ref[...]

    @pl.when(pl.program_id(0) == 0)
    def _():
        lon_out[...] = lon_ref[...]
        lat_out[...] = lat_ref[...]
        rad_out[...] = rad_ref[...]
        core_out[...] = core_ref[...]


def local(t, k, q, u, v, w):
    nl, nz = lax.axis_size("lon"), lax.axis_size("lat")
    ni, nj, nr = t.shape
    r = u.shape[1]
    rows = r * r * r // 128
    piece = rows // nl
    blocks = r * r // 128
    most = max(nl, nz)
    vm = pl.BlockSpec(memory_space=pltpu.VMEM)
    sds = lambda *s: jax.ShapeDtypeStruct(s, F32)
    V = lambda *s: pltpu.VMEM(s, F32)
    phases = 18
    small = (sds(ni, r), sds(nj, r), sds(nr, r), sds(r * r, r))
    temp, s, lon, lat, rad, core = pl.pallas_call(
        functools.partial(sweep_kernel, nl, nz),
        out_shape=(sds(ni, nj, nr), sds(ni, r, nr)) + small,
        in_specs=[vm] * 6,
        out_specs=(pl.BlockSpec(memory_space=pl.ANY),) + (vm,) * 5,
        scratch_shapes=[
            V(2, ni, nj, nr), V(ni + 1, nj, nr), V(ni, nj, nr), V(ni, nj, nr),
            V(2, ni, nr), V(STEPS + 1, 2, nj, nr), V(STEPS + 1, 2, ni, nr), V(STEPS + 1, 2, ni, nr),
            V(r, ni, nj), V(r, r, nr), V(r, r, nr),
            V(blocks, ni, 128), V(blocks, nj, 128), V(2, r, r),
            V(nz, r, ni), V(nl, r, nj), V(nl, r, nr), V(nz, r, nr),
            V(nl, r, r), V(nz, r, r),
            V(4, rows, 128), V(4, nl, piece, 128), V(4, nz, piece, 128), V(4, rows, 128),
            pltpu.SemaphoreType.DMA((phases, most)),
            pltpu.SemaphoreType.DMA((phases, most)),
            pltpu.SemaphoreType.DMA((STEPS + 1, 4)),
            pltpu.SemaphoreType.DMA((STEPS + 1, 4)),
            pltpu.SemaphoreType.DMA,
        ],
        compiler_params=pltpu.CompilerParams(
            collective_id=1, has_side_effects=True, vmem_limit_bytes=48 * 1024 * 1024
        ),
    )(t, k, q, u, v, w)
    at = 8
    slabs = lambda n: pl.BlockSpec((at, n, nr), lambda i: (i, 0, 0))
    whole = [pl.BlockSpec(x.shape, lambda i: (0, 0)) for x in small]
    temp, err, lon, lat, rad, core = pl.pallas_call(
        error_kernel,
        grid=(ni // at,),
        out_shape=(sds(ni, nj, nr), sds(ni, nj, nr)) + small,
        in_specs=[slabs(nj), slabs(r)] + whole,
        out_specs=[slabs(nj), slabs(nj)] + whole,
    )(temp, s, lon, lat, rad, core)
    return temp, err, lon, lat, rad, core.reshape(r, r, r)


def solution(mesh):
    grid = P("lon", "lat", None)
    in_specs = (grid, grid, grid, P("lon", None), P("lat", None), P())
    out_specs = (grid, grid, P("lon", None), P("lat", None), P(), P())
    return jax.shard_map(local, mesh=mesh, in_specs=in_specs, out_specs=out_specs, check_vma=False)
```

```python
import functools

import jax
import jax.numpy as jnp
from jax import lax
from jax.experimental import pallas as pl
from jax.experimental.pallas import tpu as pltpu
from jax.sharding import PartitionSpec as P

STEPS = 4
time_step = 0.15
F32 = jnp.float32
BF16 = jnp.bfloat16
NN = (((1,), (0,)), ((), ()))
NT = (((1,), (1,)), ((), ()))
TN = (((0,), (0,)), ((), ()))


def split(x):
    hi = x.astype(BF16)
    return hi, (x - hi.astype(F32)).astype(BF16)


def dot3(a, b, dims=NN):
    ah, al = a
    bh, bl = b
    d = functools.partial(lax.dot_general, dimension_numbers=dims, preferred_element_type=F32)
    return d(ah, bh) + d(ah, bl) + d(al, bh)


def mm(a, b, dims=NN):
    return dot3(split(a), split(b), dims)


def mmh(a, b, dims=NN):
    return lax.dot_general(
        a, b, dims, precision=lax.Precision.HIGHEST, preferred_element_type=F32
    )


def chol_inverse(gram):
    n = gram.shape[0]
    row = lax.broadcasted_iota(jnp.int32, (n, n), 0)
    col = lax.broadcasted_iota(jnp.int32, (n, n), 1)
    eye = jnp.where(row == col, 1.0, 0.0).astype(F32)
    m = jnp.concatenate([gram, eye], axis=1)
    rows = lax.broadcasted_iota(jnp.int32, (n, 1), 0)
    for k in range(n - 1):
        top = m[k : k + 1, :]
        factor = jnp.where(rows > k, m[:, k : k + 1] / m[k : k + 1, k : k + 1], 0.0)
        m = m - factor * top
    diag = jnp.sum(jnp.where(row == col, m[:, :n], 0.0), axis=1, keepdims=True)
    return m[:, n:] / jnp.sqrt(diag)


def block_diag(x, count):
    n = x.shape[0]
    wide = jnp.concatenate([x] * count, axis=1)
    full = jnp.concatenate([wide] * count, axis=0)
    row = lax.broadcasted_iota(jnp.int32, full.shape, 0) // n
    col = lax.broadcasted_iota(jnp.int32, full.shape, 1) // n
    return jnp.where(row == col, full, 0.0)


class Comm:
    def __init__(self, nl, nz, send_sem, recv_sem, halo_send, halo_recv):
        self.halo_send, self.halo_recv = halo_send, halo_recv
        self.nl, self.nz = nl, nz
        self.lon = lax.axis_index("lon")
        self.lat = lax.axis_index("lat")
        self.send_sem, self.recv_sem = send_sem, recv_sem
        self.phase = 0
        self.sent = []

    def start(self, axis, source, target):
        count = self.nl if axis == "lon" else self.nz
        me = self.lon if axis == "lon" else self.lat
        ph = self.phase
        self.phase += 1
        waits = []
        for d in range(1, count):
            peer = lax.rem(me + d, count)
            owner = lax.rem(me + count - d, count)
            copy = pltpu.make_async_remote_copy(
                src_ref=source(peer),
                dst_ref=target(me),
                send_sem=self.send_sem.at[ph, d],
                recv_sem=self.recv_sem.at[ph, d],
                device_id={axis: peer},
                device_id_type=pl.DeviceIdType.MESH,
            )
            copy.start()
            self.sent.append(copy)
            waits.append(
                pltpu.make_async_remote_copy(
                    src_ref=target(owner),
                    dst_ref=target(owner),
                    send_sem=self.send_sem.at[ph, d],
                    recv_sem=self.recv_sem.at[ph, d],
                    device_id={axis: peer},
                    device_id_type=pl.DeviceIdType.MESH,
                )
            )
        return waits

    def send(self, axis, shift, k, lane, source, target):
        count = self.nl if axis == "lon" else self.nz
        me = self.lon if axis == "lon" else self.lat
        return pltpu.make_async_remote_copy(
            src_ref=source,
            dst_ref=target,
            send_sem=self.halo_send.at[k, lane],
            recv_sem=self.halo_recv.at[k, lane],
            device_id={axis: lax.rem(me + shift + count, count)},
            device_id_type=pl.DeviceIdType.MESH,
        )

    def gather(self, axis, slots):
        me = self.lon if axis == "lon" else self.lat
        return self.start(axis, lambda peer: slots.at[me], lambda owner: slots.at[owner])

    def wait(self, waits):
        for w in waits:
            w.wait_recv()

    def finish(self):
        for c in self.sent:
            c.wait_send()


def total(slots):
    out = slots[0]
    for k in range(1, slots.shape[0]):
        out = out + slots[k]
    return out


def all_reduce(comm, buf, rs, zs, ag, during=None):
    rows = rs.shape[1]
    piece = lambda ref, p: ref.at[pl.ds(pl.multiple_of(p * rows, rows), rows)]
    first = comm.start("lon", lambda peer: piece(buf, peer), lambda owner: rs.at[owner])
    rs[comm.lon] = piece(buf, comm.lon)[...]
    if during is not None:
        during[0]()
    comm.wait(first)
    zs[comm.lat] = total(rs)
    second = comm.gather("lat", zs)
    if during is not None:
        during[1]()
    comm.wait(second)
    piece(ag, comm.lon)[...] = total(zs)
    third = comm.start("lon", lambda peer: piece(ag, comm.lon), lambda owner: piece(ag, owner))
    if during is not None:
        during[2]()
    comm.wait(third)


def harmonic(cond_a, cond_b):
    summed = cond_a + cond_b
    return 2.0 * cond_a * cond_b / jnp.where(summed > 0.0, summed, 1.0)


def batched(low, high, size, values, store):
    def group(first, count):
        outs = [values(first + k) for k in range(count)]
        for k, out in enumerate(outs):
            store(first + k, out)

    trips = (high - low) // size

    @pl.loop(0, trips)
    def _(trip):
        group(low + trip * size, size)

    left = high - low - trips * size
    if left:
        group(high - left, left)


def store_in(ref):
    def store(i, value):
        ref[i] = value

    return store


def conduct(comm, t0, k_ref, q_ref, ta, tb, hx, hy, hz, edge_k, hal_lon, hal_lat, pack):
    ni, nj, nr = t0.shape
    last_step = STEPS
    has_lo, has_hi = comm.lat > 0, comm.lat < comm.nz - 1

    def exchange(k, src):
        lon_copies = (
            comm.send("lon", 1, k, 0, src.at[ni - 1], hal_lon.at[k, 0]),
            comm.send("lon", -1, k, 1, src.at[0], hal_lon.at[k, 1]),
        )
        lat_copies = (
            (has_hi, has_lo, comm.send("lat", 1, k, 2, pack.at[k, 1], hal_lat.at[k, 0])),
            (has_lo, has_hi, comm.send("lat", -1, k, 3, pack.at[k, 0], hal_lat.at[k, 1])),
        )
        for c in lon_copies:
            c.start()
        for out, _, c in lat_copies:
            pl.when(out)(c.start)

        def wait():
            for c in lon_copies:
                c.wait_recv()
            for _, into, c in lat_copies:
                pl.when(into)(c.wait_recv)

        def wait_sent():
            for c in lon_copies:
                c.wait_send()
            for out, _, c in lat_copies:
                pl.when(out)(c.wait_send)

        return wait, wait_sent

    @pl.when(comm.lat == 0)
    def _():
        for k in range(STEPS + 1):
            hal_lat[k, 0] = jnp.zeros((ni, nr), F32)

    @pl.when(comm.lat == comm.nz - 1)
    def _():
        for k in range(STEPS + 1):
            hal_lat[k, 1] = jnp.zeros((ni, nr), F32)

    pack[last_step, 0] = k_ref[:, 0, :]
    pack[last_step, 1] = k_ref[:, nj - 1, :]
    pack[0, 0] = t0[:, 0, :]
    pack[0, 1] = t0[:, nj - 1, :]
    wait_k, sent_k = exchange(last_step, k_ref)
    wait_t, sent_t = exchange(0, t0)

    row = lax.broadcasted_iota(jnp.int32, (nj, nr), 0)
    col = lax.broadcasted_iota(jnp.int32, (nj, nr), 1)

    def faces(i):
        k = k_ref[i]
        return (
            jnp.where(row == 0, 0.0, harmonic(k, pltpu.roll(k, 1, 0))),
            jnp.where(col == 0, 0.0, harmonic(k, pltpu.roll(k, 1, 1))),
        )

    def store_faces(i, values):
        hy[i], hz[i] = values

    batched(0, ni, 2, faces, store_faces)
    batched(1, ni, 4, lambda i: harmonic(k_ref[i], k_ref[i - 1]), store_in(hx))
    wait_k()
    hx[0] = harmonic(k_ref[0], hal_lon[last_step, 0])
    hx[ni] = harmonic(k_ref[ni - 1], hal_lon[last_step, 1])
    edge_k[0] = harmonic(pack[last_step, 0], hal_lat[last_step, 0])
    edge_k[1] = harmonic(pack[last_step, 1], hal_lat[last_step, 1])

    def slab(i, before, here, after):
        fx = hx[i + 1] * (after - here) - hx[i] * (here - before)
        fy = hy[i] * (here - pltpu.roll(here, 1, 0))
        fz = hz[i] * (here - pltpu.roll(here, 1, 1))
        change = q_ref[i] + fx + (pltpu.roll(fy, nj - 1, 0) - fy) + (pltpu.roll(fz, nr - 1, 1) - fz)
        return here + time_step * change

    for step in range(STEPS):
        src = t0 if step == 0 else (ta, tb)[(step - 1) % 2]
        dst = (ta, tb)[step % 2]

        batched(1, ni - 1, 4, lambda i: slab(i, src[i - 1], src[i], src[i + 1]), store_in(dst))

        wait_t()
        dst[0] = slab(0, hal_lon[step, 0], src[0], src[1])
        dst[ni - 1] = slab(ni - 1, src[ni - 2], src[ni - 1], hal_lon[step, 1])
        for side, j in ((0, 0), (1, nj - 1)):
            flux = edge_k[side] * (hal_lat[step, side] - pack[step, side])
            edge = dst[:, j, :] + time_step * flux
            dst[:, j, :] = edge
            if step < STEPS - 1:
                pack[step + 1, side] = edge
        sent_t()
        if step < STEPS - 1:
            wait_t, sent_t = exchange(step + 1, dst)
    sent_k()


def sweep_kernel(nl, nz, t0, k_ref, q_ref, u_ref, v_ref, w_ref,
                 temp_ref, x3, lon_ref, lat_ref, rad_ref, core_ref,
                 ta, tb, hx, hy, hz, edge_k, hal_lon, hal_lat, pack,
                 z1, y3, f_ref, y1, y2, small,
                 b1s, b2s, b3l, b3z, g1s, g2s, bufs, rss, zss, ags,
                 send_sem, recv_sem, halo_send, halo_recv, out_sem):
    comm = Comm(nl, nz, send_sem, recv_sem, halo_send, halo_recv)
    ni, nj, nr = t0.shape
    t_ref = (ta, tb)[(STEPS - 1) % 2]
    r = u_ref.shape[0]
    group = 128 // r
    blocks = r // group

    barrier = pltpu.get_barrier_semaphore()
    for d in range(1, nl):
        pl.semaphore_signal(barrier, inc=1, device_id={"lon": lax.rem(comm.lon + d, nl)},
                            device_id_type=pl.DeviceIdType.MESH)
    for d in range(1, nz):
        pl.semaphore_signal(barrier, inc=1, device_id={"lat": lax.rem(comm.lat + d, nz)},
                            device_id_type=pl.DeviceIdType.MESH)

    pl.semaphore_wait(barrier, nl + nz - 2)
    conduct(comm, t0, k_ref, q_ref, ta, tb, hx, hy, hz, edge_k, hal_lon, hal_lat, pack)
    out_copy = pltpu.make_async_copy(t_ref, temp_ref, out_sem)
    out_copy.start()

    wts = split(w_ref[...])
    ut = u_ref[...]
    vt = v_ref[...]

    def store_z1(i, value):
        z1[:, i, :] = value

    batched(0, ni, 8, lambda i: dot3(wts, split(t_ref[i]), NT), store_z1)

    lane = lambda n: lax.broadcasted_iota(jnp.int32, (n, 128), 1) // r
    v4 = split(jnp.concatenate([vt.T] * group, axis=1))
    uts = split(ut)
    for m in range(blocks):
        out = jnp.zeros((ni, 128), F32)
        for g in range(group):
            out = jnp.where(lane(ni) == g, dot3(split(z1[m * group + g]), v4), out)
        y1[m] = out
        bufs[0, pl.ds(m * r, r), :] = dot3(uts, split(out))

    all_reduce(comm, bufs.at[0], rss.at[0], zss.at[0], ags.at[0])

    acc = jnp.zeros((r, ni), F32)
    for m in range(blocks):
        acc = acc + mm(ags[0, pl.ds(m * r, r), :], y1[m], NT)
    b1s[comm.lat] = acc
    w = comm.gather("lat", b1s)
    comm.wait(w)
    b1t = total(b1s)
    g1s[comm.lon] = mmh(b1t, b1t, NT)
    g1w = comm.gather("lon", g1s)
    b1x = split(jnp.concatenate([b1t] * group, axis=0).T)
    vts = split(vt)
    for m in range(blocks):
        out = jnp.zeros((nj, 128), F32)
        for g in range(group):
            out = jnp.where(lane(nj) == g, dot3(split(z1[m * group + g]), b1x, TN), out)
        y2[m] = out
        bufs[1, pl.ds(m * r, r), :] = dot3(vts, split(out))

    def chol1():
        comm.wait(g1w)
        small[0] = chol_inverse(total(g1s))

    nothing = lambda: None
    all_reduce(comm, bufs.at[1], rss.at[1], zss.at[1], ags.at[1], (nothing, chol1, nothing))

    l1 = small[0]
    bd1 = split(block_diag(mmh(l1, l1, TN), group))
    acc = jnp.zeros((r, nj), F32)
    for m in range(blocks):
        acc = acc + mm(dot3(split(ags[1, pl.ds(m * r, r), :]), bd1), y2[m], NT)
    b2s[comm.lon] = acc
    w = comm.gather("lon", b2s)
    lont = mmh(l1, b1t)
    lon_ref[...] = lont
    comm.wait(w)
    b2t = total(b2s)
    g2s[comm.lat] = mmh(b2t, b2t, NT)
    g2w = comm.gather("lat", g2s)
    b2h = split(b2t)

    batched(0, ni, 8, lambda i: dot3(b2h, split(t_ref[i])), store_in(x3))

    lonh = split(lont)
    for b in range(r):
        y3[:, b, :] = dot3(lonh, split(x3[:, b, :]))

    per = 128 // r

    def y3block(m):
        return split(y3[pl.ds(m * per, per)].reshape(128, nr))

    for m in range(blocks):
        bufs[2, pl.ds(m * r, r), :] = dot3(wts, y3block(m), NT)

    def chol2():
        comm.wait(g2w)
        small[1] = chol_inverse(total(g2s))

    all_reduce(comm, bufs.at[2], rss.at[2], zss.at[2], ags.at[2], (chol2, nothing, nothing))

    l2 = small[1]
    bd2 = split(block_diag(mmh(l2, l2, TN), group))
    acc = jnp.zeros((r, nr), F32)
    for m in range(blocks):
        acc = acc + dot3(split(dot3(split(ags[2, pl.ds(m * r, r), :]), bd2)), y3block(m))
    b3l[comm.lon] = acc
    w = comm.gather("lon", b3l)
    latt = mmh(l2, b2t)
    lat_ref[...] = latt
    comm.wait(w)
    b3z[comm.lat] = total(b3l)
    w = comm.gather("lat", b3z)
    comm.wait(w)
    b3t = total(b3z)
    l3 = chol_inverse(mmh(b3t, b3t, NT))
    radt = mmh(l3, b3t)
    rad_ref[...] = radt
    radh = split(radt)
    for m in range(blocks):
        bufs[3, pl.ds(m * r, r), :] = dot3(radh, y3block(m), NT)
    all_reduce(comm, bufs.at[3], rss.at[3], zss.at[3], ags.at[3])

    bdl = split(block_diag(l2.T, group))
    for m in range(blocks):
        core = dot3(split(ags[3, pl.ds(m * r, r), :]), bdl)
        core_ref[pl.ds(m * 128, 128), :] = core.T
        f_ref[pl.ds(m * per, per)] = dot3(split(core), radh, TN).reshape(per, r, nr)
    lonb = split(lont.T)
    for b in range(r):
        x3[:, b, :] = dot3(lonb, split(f_ref[:, b, :]))
    out_copy.wait()
    comm.finish()


def error_kernel(t_ref, s_ref, lon_ref, lat_ref, rad_ref, core_ref,
                 temp_out, err_out, lon_out, lat_out, rad_out, core_out, err, sem, temp_sem):
    temp_copy = pltpu.make_async_copy(t_ref, temp_out, temp_sem)
    temp_copy.start()
    latb = split(lat_ref[...].T)
    ni = t_ref.shape[0]
    at = 8

    def chunk(c):
        part = pl.ds(c * at, at)
        return pltpu.make_async_copy(err.at[part], err_out.at[part], sem.at[c])

    @pl.loop(0, ni // at)
    def _(c):
        outs = [t_ref[c * at + k] - dot3(latb, split(s_ref[c * at + k])) for k in range(at)]
        for k, out in enumerate(outs):
            err[c * at + k] = out
        chunk(c).start()

    lon_out[...] = lon_ref[...]
    lat_out[...] = lat_ref[...]
    rad_out[...] = rad_ref[...]
    core_out[...] = core_ref[...]

    @pl.loop(0, ni // at)
    def _(c):
        chunk(c).wait()

    temp_copy.wait()


def local(t, k, q, u, v, w):
    nl, nz = lax.axis_size("lon"), lax.axis_size("lat")
    ni, nj, nr = t.shape
    r = u.shape[1]
    rows = r * r * r // 128
    piece = rows // nl
    blocks = r * r // 128
    most = max(nl, nz)
    vm = pl.BlockSpec(memory_space=pltpu.VMEM)
    sds = lambda *s: jax.ShapeDtypeStruct(s, F32)
    V = lambda *s: pltpu.VMEM(s, F32)
    phases = 18
    small = (sds(r, ni), sds(r, nj), sds(r, nr), sds(r * r, r))
    temp, s, lon, lat, rad, core = pl.pallas_call(
        functools.partial(sweep_kernel, nl, nz),
        out_shape=(sds(ni, nj, nr), sds(ni, r, nr)) + small,
        in_specs=[vm] * 6,
        out_specs=(pl.BlockSpec(memory_space=pl.ANY),) + (vm,) * 5,
        scratch_shapes=[
            V(ni, nj, nr), V(ni, nj, nr), V(ni + 1, nj, nr), V(ni, nj, nr), V(ni, nj, nr),
            V(2, ni, nr), V(STEPS + 1, 2, nj, nr), V(STEPS + 1, 2, ni, nr), V(STEPS + 1, 2, ni, nr),
            V(r, ni, nj), V(r, r, nr), V(r, r, nr),
            V(blocks, ni, 128), V(blocks, nj, 128), V(2, r, r),
            V(nz, r, ni), V(nl, r, nj), V(nl, r, nr), V(nz, r, nr),
            V(nl, r, r), V(nz, r, r),
            V(4, rows, 128), V(4, nl, piece, 128), V(4, nz, piece, 128), V(4, rows, 128),
            pltpu.SemaphoreType.DMA((phases, most)),
            pltpu.SemaphoreType.DMA((phases, most)),
            pltpu.SemaphoreType.DMA((STEPS + 1, 4)),
            pltpu.SemaphoreType.DMA((STEPS + 1, 4)),
            pltpu.SemaphoreType.DMA,
        ],
        compiler_params=pltpu.CompilerParams(
            collective_id=1, has_side_effects=True, vmem_limit_bytes=48 * 1024 * 1024
        ),
    )(t, k, q, u.T, v.T, w.T)
    anywhere = pl.BlockSpec(memory_space=pl.ANY)
    temp, err, lon, lat, rad, core = pl.pallas_call(
        error_kernel,
        out_shape=(sds(ni, nj, nr), sds(ni, nj, nr)) + small,
        in_specs=[vm] * 6,
        out_specs=(anywhere, anywhere) + (vm,) * 4,
        scratch_shapes=[
            V(ni, nj, nr), pltpu.SemaphoreType.DMA((ni // 8,)), pltpu.SemaphoreType.DMA
        ],
        compiler_params=pltpu.CompilerParams(vmem_limit_bytes=12 * 1024 * 1024),
    )(temp, s, lon, lat, rad, core)
    return temp, err, lon.T, lat.T, rad.T, core.reshape(r, r, r)


def solution(mesh):
    grid = P("lon", "lat", None)
    in_specs = (grid, grid, grid, P("lon", None), P("lat", None), P())
    out_specs = (grid, grid, P("lon", None), P("lat", None), P(), P())
    return jax.shard_map(local, mesh=mesh, in_specs=in_specs, out_specs=out_specs, check_vma=False)
```

```python
import functools

import jax
import jax.numpy as jnp
from jax import lax
from jax.experimental import pallas as pl
from jax.experimental.pallas import tpu as pltpu
from jax.sharding import PartitionSpec as P

STEPS = 4
time_step = 0.15
F32 = jnp.float32
BF16 = jnp.bfloat16
NN = (((1,), (0,)), ((), ()))
NT = (((1,), (1,)), ((), ()))
TN = (((0,), (0,)), ((), ()))


def split(x):
    hi = x.astype(BF16)
    return hi, (x - hi.astype(F32)).astype(BF16)


def dot3(a, b, dims=NN):
    ah, al = a
    bh, bl = b
    d = functools.partial(lax.dot_general, dimension_numbers=dims, preferred_element_type=F32)
    return d(ah, bh) + d(ah, bl) + d(al, bh)


def mm(a, b, dims=NN):
    return dot3(split(a), split(b), dims)


def mmh(a, b, dims=NN):
    return lax.dot_general(
        a, b, dims, precision=lax.Precision.HIGHEST, preferred_element_type=F32
    )


def chol_inverse(gram):
    n = gram.shape[0]
    row = lax.broadcasted_iota(jnp.int32, (n, n), 0)
    col = lax.broadcasted_iota(jnp.int32, (n, n), 1)
    eye = jnp.where(row == col, 1.0, 0.0).astype(F32)
    m = jnp.concatenate([gram, eye], axis=1)
    rows = lax.broadcasted_iota(jnp.int32, (n, 1), 0)
    for k in range(n - 1):
        top = m[k : k + 1, :]
        factor = jnp.where(rows > k, m[:, k : k + 1] / m[k : k + 1, k : k + 1], 0.0)
        m = m - factor * top
    diag = jnp.sum(jnp.where(row == col, m[:, :n], 0.0), axis=1, keepdims=True)
    return m[:, n:] / jnp.sqrt(diag)


def block_diag(x, count):
    n = x.shape[0]
    wide = jnp.concatenate([x] * count, axis=1)
    full = jnp.concatenate([wide] * count, axis=0)
    row = lax.broadcasted_iota(jnp.int32, full.shape, 0) // n
    col = lax.broadcasted_iota(jnp.int32, full.shape, 1) // n
    return jnp.where(row == col, full, 0.0)


class Comm:
    def __init__(self, nl, nz, send_sem, recv_sem, halo_send, halo_recv):
        self.halo_send, self.halo_recv = halo_send, halo_recv
        self.nl, self.nz = nl, nz
        self.lon = lax.axis_index("lon")
        self.lat = lax.axis_index("lat")
        self.send_sem, self.recv_sem = send_sem, recv_sem
        self.phase = 0
        self.sent = []

    def start(self, axis, source, target):
        count = self.nl if axis == "lon" else self.nz
        me = self.lon if axis == "lon" else self.lat
        ph = self.phase
        self.phase += 1
        waits = []
        for d in range(1, count):
            peer = lax.rem(me + d, count)
            owner = lax.rem(me + count - d, count)
            copy = pltpu.make_async_remote_copy(
                src_ref=source(peer),
                dst_ref=target(me),
                send_sem=self.send_sem.at[ph, d],
                recv_sem=self.recv_sem.at[ph, d],
                device_id={axis: peer},
                device_id_type=pl.DeviceIdType.MESH,
            )
            copy.start()
            self.sent.append(copy)
            waits.append(
                pltpu.make_async_remote_copy(
                    src_ref=target(owner),
                    dst_ref=target(owner),
                    send_sem=self.send_sem.at[ph, d],
                    recv_sem=self.recv_sem.at[ph, d],
                    device_id={axis: peer},
                    device_id_type=pl.DeviceIdType.MESH,
                )
            )
        return waits

    def send(self, axis, shift, k, lane, source, target):
        count = self.nl if axis == "lon" else self.nz
        me = self.lon if axis == "lon" else self.lat
        return pltpu.make_async_remote_copy(
            src_ref=source,
            dst_ref=target,
            send_sem=self.halo_send.at[k, lane],
            recv_sem=self.halo_recv.at[k, lane],
            device_id={axis: lax.rem(me + shift + count, count)},
            device_id_type=pl.DeviceIdType.MESH,
        )

    def gather(self, axis, slots):
        me = self.lon if axis == "lon" else self.lat
        return self.start(axis, lambda peer: slots.at[me], lambda owner: slots.at[owner])

    def wait(self, waits):
        for w in waits:
            w.wait_recv()

    def finish(self):
        for c in self.sent:
            c.wait_send()


def total(slots):
    out = slots[0]
    for k in range(1, slots.shape[0]):
        out = out + slots[k]
    return out


def all_reduce(comm, buf, rs, zs, ag, during=None):
    rows = rs.shape[1]
    piece = lambda ref, p: ref.at[pl.ds(pl.multiple_of(p * rows, rows), rows)]
    first = comm.start("lon", lambda peer: piece(buf, peer), lambda owner: rs.at[owner])
    rs[comm.lon] = piece(buf, comm.lon)[...]
    if during is not None:
        during[0]()
    comm.wait(first)
    zs[comm.lat] = total(rs)
    second = comm.gather("lat", zs)
    if during is not None:
        during[1]()
    comm.wait(second)
    piece(ag, comm.lon)[...] = total(zs)
    third = comm.start("lon", lambda peer: piece(ag, comm.lon), lambda owner: piece(ag, owner))
    if during is not None:
        during[2]()
    comm.wait(third)


def harmonic(cond_a, cond_b):
    summed = cond_a + cond_b
    return 2.0 * cond_a * cond_b / jnp.where(summed > 0.0, summed, 1.0)


def batched(low, high, size, values, store):
    def group(first, count):
        outs = [values(first + k) for k in range(count)]
        for k, out in enumerate(outs):
            store(first + k, out)

    trips = (high - low) // size

    @pl.loop(0, trips)
    def _(trip):
        group(low + trip * size, size)

    left = high - low - trips * size
    if left:
        group(high - left, left)


def store_in(ref):
    def store(i, value):
        ref[i] = value

    return store


def conduct(comm, t0, k_ref, q_ref, ta, tb, hx, hy, hz, edge_k, hal_lon, hal_lat, pack):
    ni, nj, nr = t0.shape
    last_step = STEPS
    has_lo, has_hi = comm.lat > 0, comm.lat < comm.nz - 1

    def exchange(k, src):
        lon_copies = (
            comm.send("lon", 1, k, 0, src.at[ni - 1], hal_lon.at[k, 0]),
            comm.send("lon", -1, k, 1, src.at[0], hal_lon.at[k, 1]),
        )
        lat_copies = (
            (has_hi, has_lo, comm.send("lat", 1, k, 2, pack.at[k, 1], hal_lat.at[k, 0])),
            (has_lo, has_hi, comm.send("lat", -1, k, 3, pack.at[k, 0], hal_lat.at[k, 1])),
        )
        for c in lon_copies:
            c.start()
        for out, _, c in lat_copies:
            pl.when(out)(c.start)

        def wait():
            for c in lon_copies:
                c.wait_recv()
            for _, into, c in lat_copies:
                pl.when(into)(c.wait_recv)

        def wait_sent():
            for c in lon_copies:
                c.wait_send()
            for out, _, c in lat_copies:
                pl.when(out)(c.wait_send)

        return wait, wait_sent

    @pl.when(comm.lat == 0)
    def _():
        for k in range(STEPS + 1):
            hal_lat[k, 0] = jnp.zeros((ni, nr), F32)

    @pl.when(comm.lat == comm.nz - 1)
    def _():
        for k in range(STEPS + 1):
            hal_lat[k, 1] = jnp.zeros((ni, nr), F32)

    pack[last_step, 0] = k_ref[:, 0, :]
    pack[last_step, 1] = k_ref[:, nj - 1, :]
    pack[0, 0] = t0[:, 0, :]
    pack[0, 1] = t0[:, nj - 1, :]
    wait_k, sent_k = exchange(last_step, k_ref)
    wait_t, sent_t = exchange(0, t0)

    row = lax.broadcasted_iota(jnp.int32, (nj, nr), 0)
    col = lax.broadcasted_iota(jnp.int32, (nj, nr), 1)

    def faces(i):
        k = k_ref[i]
        return (
            jnp.where(row == 0, 0.0, harmonic(k, pltpu.roll(k, 1, 0))),
            jnp.where(col == 0, 0.0, harmonic(k, pltpu.roll(k, 1, 1))),
        )

    def store_faces(i, values):
        hy[i], hz[i] = values

    batched(0, ni, 2, faces, store_faces)
    batched(1, ni, 4, lambda i: harmonic(k_ref[i], k_ref[i - 1]), store_in(hx))
    wait_k()
    hx[0] = harmonic(k_ref[0], hal_lon[last_step, 0])
    hx[ni] = harmonic(k_ref[ni - 1], hal_lon[last_step, 1])
    edge_k[0] = harmonic(pack[last_step, 0], hal_lat[last_step, 0])
    edge_k[1] = harmonic(pack[last_step, 1], hal_lat[last_step, 1])

    def slab(i, before, here, after):
        fx = hx[i + 1] * (after - here) - hx[i] * (here - before)
        fy = hy[i] * (here - pltpu.roll(here, 1, 0))
        fz = hz[i] * (here - pltpu.roll(here, 1, 1))
        change = q_ref[i] + fx + (pltpu.roll(fy, nj - 1, 0) - fy) + (pltpu.roll(fz, nr - 1, 1) - fz)
        return here + time_step * change

    for step in range(STEPS):
        src = t0 if step == 0 else (ta, tb)[(step - 1) % 2]
        dst = (ta, tb)[step % 2]

        batched(1, ni - 1, 4, lambda i: slab(i, src[i - 1], src[i], src[i + 1]), store_in(dst))

        wait_t()
        dst[0] = slab(0, hal_lon[step, 0], src[0], src[1])
        dst[ni - 1] = slab(ni - 1, src[ni - 2], src[ni - 1], hal_lon[step, 1])
        for side, j in ((0, 0), (1, nj - 1)):
            flux = edge_k[side] * (hal_lat[step, side] - pack[step, side])
            edge = dst[:, j, :] + time_step * flux
            dst[:, j, :] = edge
            if step < STEPS - 1:
                pack[step + 1, side] = edge
        sent_t()
        if step < STEPS - 1:
            wait_t, sent_t = exchange(step + 1, dst)
    sent_k()


def sweep_kernel(nl, nz, t0, k_ref, q_ref, u_ref, v_ref, w_ref,
                 temp_ref, x3, lon_ref, lat_ref, rad_ref, core_ref,
                 ta, tb, hx, hy, hz, edge_k, hal_lon, hal_lat, pack,
                 z1, z1t, y3h, y3, f_ref, y1, y2, small,
                 b1s, b2s, b3l, b3z, g1s, g2s, bufs, rss, zss, ags,
                 send_sem, recv_sem, halo_send, halo_recv, out_sem):
    comm = Comm(nl, nz, send_sem, recv_sem, halo_send, halo_recv)
    ni, nj, nr = t0.shape
    t_ref = (ta, tb)[(STEPS - 1) % 2]
    r = u_ref.shape[0]
    group = 128 // r
    blocks = r // group

    barrier = pltpu.get_barrier_semaphore()
    for d in range(1, nl):
        pl.semaphore_signal(barrier, inc=1, device_id={"lon": lax.rem(comm.lon + d, nl)},
                            device_id_type=pl.DeviceIdType.MESH)
    for d in range(1, nz):
        pl.semaphore_signal(barrier, inc=1, device_id={"lat": lax.rem(comm.lat + d, nz)},
                            device_id_type=pl.DeviceIdType.MESH)

    pl.semaphore_wait(barrier, nl + nz - 2)
    conduct(comm, t0, k_ref, q_ref, ta, tb, hx, hy, hz, edge_k, hal_lon, hal_lat, pack)
    out_copy = pltpu.make_async_copy(t_ref, temp_ref, out_sem)
    out_copy.start()

    wts = split(w_ref[...])
    ut = u_ref[...]
    vt = v_ref[...]

    def store_z1(i, value):
        z1[:, i, :] = value

    batched(0, ni, 8, lambda i: dot3(wts, split(t_ref[i]), NT), store_z1)

    lane = lambda n: lax.broadcasted_iota(jnp.int32, (n, 128), 1) // r
    v4 = split(jnp.concatenate([vt.T] * group, axis=1))
    uts = split(ut)
    for m in range(blocks):
        out = jnp.zeros((ni, 128), F32)
        for g in range(group):
            out = jnp.where(lane(ni) == g, dot3(split(z1[m * group + g]), v4), out)
        y1[m] = out
        bufs[0, pl.ds(m * r, r), :] = dot3(uts, split(out))

    def turn(low, high):
        for b in range(low, high):
            z1t[b] = z1[b].T

    turns = tuple(functools.partial(turn, r * k // 3, r * (k + 1) // 3) for k in range(3))
    all_reduce(comm, bufs.at[0], rss.at[0], zss.at[0], ags.at[0], turns)

    acc = jnp.zeros((r, ni), F32)
    for m in range(blocks):
        acc = acc + mm(ags[0, pl.ds(m * r, r), :], y1[m], NT)
    b1s[comm.lat] = acc
    w = comm.gather("lat", b1s)
    comm.wait(w)
    b1t = total(b1s)
    g1s[comm.lon] = mmh(b1t, b1t, NT)
    g1w = comm.gather("lon", g1s)
    b1x = split(jnp.concatenate([b1t] * group, axis=0).T)
    vts = split(vt)
    for m in range(blocks):
        out = jnp.zeros((nj, 128), F32)
        for g in range(group):
            out = jnp.where(lane(nj) == g, dot3(split(z1t[m * group + g]), b1x), out)
        y2[m] = out
        bufs[1, pl.ds(m * r, r), :] = dot3(vts, split(out))

    def chol1():
        comm.wait(g1w)
        small[0] = chol_inverse(total(g1s))

    nothing = lambda: None
    all_reduce(comm, bufs.at[1], rss.at[1], zss.at[1], ags.at[1], (nothing, chol1, nothing))

    l1 = small[0]
    bd1 = split(block_diag(mmh(l1, l1, TN), group))
    acc = jnp.zeros((r, nj), F32)
    for m in range(blocks):
        acc = acc + mm(dot3(split(ags[1, pl.ds(m * r, r), :]), bd1), y2[m], NT)
    b2s[comm.lon] = acc
    w = comm.gather("lon", b2s)
    lont = mmh(l1, b1t)
    lon_ref[...] = lont
    comm.wait(w)
    b2t = total(b2s)
    g2s[comm.lat] = mmh(b2t, b2t, NT)
    g2w = comm.gather("lat", g2s)
    b2h = split(b2t)

    batched(0, ni, 8, lambda i: dot3(b2h, split(t_ref[i])), store_in(x3))

    lonh = split(lont)
    for b in range(r):
        y3[:, b, :] = dot3(lonh, split(x3[:, b, :]))

    per = 128 // r

    def y3block(m):
        return split(y3[pl.ds(m * per, per)].reshape(128, nr))

    for m in range(blocks):
        high, low = y3block(m)
        y3h[0, pl.ds(m * 128, 128), :] = high
        y3h[1, pl.ds(m * 128, 128), :] = low
        bufs[2, pl.ds(m * r, r), :] = dot3(wts, (high, low), NT)

    def y3kept(m):
        return y3h[0, pl.ds(m * 128, 128), :], y3h[1, pl.ds(m * 128, 128), :]

    def chol2():
        comm.wait(g2w)
        small[1] = chol_inverse(total(g2s))

    all_reduce(comm, bufs.at[2], rss.at[2], zss.at[2], ags.at[2], (chol2, nothing, nothing))

    l2 = small[1]
    bd2 = split(block_diag(mmh(l2, l2, TN), group))
    acc = jnp.zeros((r, nr), F32)
    for m in range(blocks):
        acc = acc + dot3(split(dot3(split(ags[2, pl.ds(m * r, r), :]), bd2)), y3kept(m))
    b3l[comm.lon] = acc
    w = comm.gather("lon", b3l)
    latt = mmh(l2, b2t)
    lat_ref[...] = latt
    comm.wait(w)
    b3z[comm.lat] = total(b3l)
    w = comm.gather("lat", b3z)
    comm.wait(w)
    b3t = total(b3z)
    l3 = chol_inverse(mmh(b3t, b3t, NT))
    radt = mmh(l3, b3t)
    rad_ref[...] = radt
    radh = split(radt)
    for m in range(blocks):
        bufs[3, pl.ds(m * r, r), :] = dot3(radh, y3kept(m), NT)
    all_reduce(comm, bufs.at[3], rss.at[3], zss.at[3], ags.at[3])

    bdl = split(block_diag(l2.T, group))
    for m in range(blocks):
        core = dot3(split(ags[3, pl.ds(m * r, r), :]), bdl)
        core_ref[pl.ds(m * 128, 128), :] = core.T
        f_ref[pl.ds(m * per, per)] = dot3(split(core), radh, TN).reshape(per, r, nr)
    lonb = split(lont.T)
    for b in range(r):
        x3[:, b, :] = dot3(lonb, split(f_ref[:, b, :]))
    out_copy.wait()
    comm.finish()


def error_kernel(t_ref, s_ref, lon_ref, lat_ref, rad_ref, core_ref,
                 temp_out, err_out, lon_out, lat_out, rad_out, core_out, err, sem, temp_sem):
    temp_copy = pltpu.make_async_copy(t_ref, temp_out, temp_sem)
    temp_copy.start()
    latb = split(lat_ref[...].T)
    ni = t_ref.shape[0]
    at = 8

    def chunk(c):
        part = pl.ds(c * at, at)
        return pltpu.make_async_copy(err.at[part], err_out.at[part], sem.at[c])

    @pl.loop(0, ni // at)
    def _(c):
        outs = [t_ref[c * at + k] - dot3(latb, split(s_ref[c * at + k])) for k in range(at)]
        for k, out in enumerate(outs):
            err[c * at + k] = out
        chunk(c).start()

    lon_out[...] = lon_ref[...]
    lat_out[...] = lat_ref[...]
    rad_out[...] = rad_ref[...]
    core_out[...] = core_ref[...]

    @pl.loop(0, ni // at)
    def _(c):
        chunk(c).wait()

    temp_copy.wait()


def local(t, k, q, u, v, w):
    nl, nz = lax.axis_size("lon"), lax.axis_size("lat")
    ni, nj, nr = t.shape
    r = u.shape[1]
    rows = r * r * r // 128
    piece = rows // nl
    blocks = r * r // 128
    most = max(nl, nz)
    vm = pl.BlockSpec(memory_space=pltpu.VMEM)
    sds = lambda *s: jax.ShapeDtypeStruct(s, F32)
    V = lambda *s: pltpu.VMEM(s, F32)
    phases = 18
    small = (sds(r, ni), sds(r, nj), sds(r, nr), sds(r * r, r))
    temp, s, lon, lat, rad, core = pl.pallas_call(
        functools.partial(sweep_kernel, nl, nz),
        out_shape=(sds(ni, nj, nr), sds(ni, r, nr)) + small,
        in_specs=[vm] * 6,
        out_specs=(pl.BlockSpec(memory_space=pl.ANY),) + (vm,) * 5,
        scratch_shapes=[
            V(ni, nj, nr), V(ni, nj, nr), V(ni + 1, nj, nr), V(ni, nj, nr), V(ni, nj, nr),
            V(2, ni, nr), V(STEPS + 1, 2, nj, nr), V(STEPS + 1, 2, ni, nr), V(STEPS + 1, 2, ni, nr),
            V(r, ni, nj), V(r, nj, ni), pltpu.VMEM((2, r * r, nr), BF16), V(r, r, nr), V(r, r, nr),
            V(blocks, ni, 128), V(blocks, nj, 128), V(2, r, r),
            V(nz, r, ni), V(nl, r, nj), V(nl, r, nr), V(nz, r, nr),
            V(nl, r, r), V(nz, r, r),
            V(4, rows, 128), V(4, nl, piece, 128), V(4, nz, piece, 128), V(4, rows, 128),
            pltpu.SemaphoreType.DMA((phases, most)),
            pltpu.SemaphoreType.DMA((phases, most)),
            pltpu.SemaphoreType.DMA((STEPS + 1, 4)),
            pltpu.SemaphoreType.DMA((STEPS + 1, 4)),
            pltpu.SemaphoreType.DMA,
        ],
        compiler_params=pltpu.CompilerParams(
            collective_id=1, has_side_effects=True, vmem_limit_bytes=48 * 1024 * 1024
        ),
    )(t, k, q, u.T, v.T, w.T)
    anywhere = pl.BlockSpec(memory_space=pl.ANY)
    temp, err, lon, lat, rad, core = pl.pallas_call(
        error_kernel,
        out_shape=(sds(ni, nj, nr), sds(ni, nj, nr)) + small,
        in_specs=[vm] * 6,
        out_specs=(anywhere, anywhere) + (vm,) * 4,
        scratch_shapes=[
            V(ni, nj, nr), pltpu.SemaphoreType.DMA((ni // 8,)), pltpu.SemaphoreType.DMA
        ],
        compiler_params=pltpu.CompilerParams(vmem_limit_bytes=12 * 1024 * 1024),
    )(temp, s, lon, lat, rad, core)
    return temp, err, lon.T, lat.T, rad.T, core.reshape(r, r, r)


def solution(mesh):
    grid = P("lon", "lat", None)
    in_specs = (grid, grid, grid, P("lon", None), P("lat", None), P())
    out_specs = (grid, grid, P("lon", None), P("lat", None), P(), P())
    return jax.shard_map(local, mesh=mesh, in_specs=in_specs, out_specs=out_specs, check_vma=False)
```
